256 devices in a mesh: aux: 16 (over x, y), occ: 16 (over z, core).
Axes of the slice: x: 4, y: 4, z: 8, core: 2. Of those that a mesh axis runs over, the one named last changes fastest.
Arguments:
- integrals: bfloat16 [32, 384, 128, 128], P('aux', 'occ'), may hold values from -1.5 to 1.5
- coefficients: bfloat16 [4096, 384], P('occ'), may hold values from -0.21875 to 0.21875
- pair_rows: int32 [16, 384], P('aux', 'occ'), may hold values from 0 to 1
- pair_cols: int32 [16, 384], P('aux', 'occ'), may hold values from 0 to 31
- pair_count: int32 [16, 16], P('aux', 'occ'), may hold values from 1 to 24, as said below
- row_blocks: int32 [32], replicated, may hold values from 0 to 31, each once
Outputs:
- exchange_matrix: float32 [4096, 4096], P('aux', 'occ')
The draws below stay inside these ranges and needn't reach their ends.
Inputs may be any that keep to these rules, and one draw needn't show every extreme that they name: `pair_count`: at most 24 live slots for each auxiliary block and row owner, and some auxiliary block and owner has exactly 24.
All inputs are finite; a program needn't handle non-finite values.
Results may differ from the reference program's by a relative error of at most 0.0022.
Values may be sent and summed in bfloat16 or wider, within the bound.
A program may use at most 64 MiB of HBM per device.

```python
import jax
import jax.numpy as jnp
from jax import lax

BS = 128
NBLK = 32
O = 384
PAIRS_DEV = 24
AUX_DEV = 2
NBAS = 4096
RB = 2
AUXBLK = 16
OCCBLK = 16
NAUX = 32


def draw_pair_count(key, part):
    first, second = jax.random.split(key)
    counts = jax.random.randint(first, (AUXBLK * OCCBLK,), 1, PAIRS_DEV + 1)
    chosen = jax.random.randint(second, (), 0, AUXBLK * OCCBLK)
    counts = jnp.where(jnp.arange(AUXBLK * OCCBLK) == chosen, PAIRS_DEV, counts)
    return counts.reshape(AUXBLK, OCCBLK).astype(jnp.int32)


def place_ends(drawn, rng, low, top_value):
    longest = drawn.shape.index(max(drawn.shape))
    spots = []
    for shift in (0, 1):
        where = [jax.random.randint(jax.random.fold_in(rng, axis), (), 0, length) for axis, length in enumerate(drawn.shape)]
        where[longest] = (where[longest] + shift) % drawn.shape[longest]
        spots.append(tuple(where))
    return drawn.at[spots[0]].set(low).at[spots[1]].set(top_value)


def steps_of(stream_key, shape, pieces, least, high):
    def one(dim, shards_of):
        heights = jax.random.uniform(jax.random.fold_in(jax.random.fold_in(stream_key, 6), dim), (shards_of,), jnp.float32, least / len(pieces), high / len(pieces))
        return jnp.repeat(jnp.exp(heights), shape[dim] // shards_of).reshape((-1,) + (1,) * (len(shape) - dim - 1))

    loudness = one(*pieces[0])
    for cut in pieces[1:]:
        loudness = loudness * one(*cut)
    return loudness


def centred(stream_key, dims, deviation, most, shards=(), held_as=jnp.bfloat16):
    values = jax.random.normal(stream_key, dims, jnp.float32) * deviation
    if len(shards) > 0:
        values = steps_of(stream_key, dims, shards, -0.22, 0.18) * values
    return jnp.clip(values, min=-most, max=most).astype(held_as)


def setup_inputs(seed: int = 0) -> dict:
    splits = jax.random.split(jax.random.key(seed), 7)
    return {
        "integrals": centred(splits[0], (NAUX, PAIRS_DEV * OCCBLK, BS, BS), ((NAUX * O) ** -0.25), 1.5, ((0, 16), (1, 16))),
        "coefficients": centred(splits[1], (NBAS, O), (BS * PAIRS_DEV // (2 * RB)) ** -0.5, 0.21875, ((0, 16),)),
        "pair_rows": place_ends(jax.random.randint(splits[2], (AUXBLK, PAIRS_DEV * OCCBLK), 0, RB), jax.random.fold_in(splits[2], 1), 0, RB - 1).astype(jnp.int32),
        "pair_cols": place_ends(jax.random.randint(splits[3], (AUXBLK, PAIRS_DEV * OCCBLK), 0, NBLK), jax.random.fold_in(splits[3], 1), 0, NBLK - 1).astype(jnp.int32),
        "pair_count": draw_pair_count(jax.random.fold_in(splits[6], 71), 0),
        "row_blocks": jax.random.permutation(splits[5], NBLK).astype(jnp.int32),
    }


def reference(integrals, coefficients, pair_rows, pair_cols, pair_count, row_blocks):
    coeff_blocks = coefficients.reshape(NBLK, BS, O).astype(jnp.float32)
    slot_index = jnp.arange(PAIRS_DEV * OCCBLK, dtype=jnp.int32)
    owner = slot_index // PAIRS_DEV
    position = slot_index % PAIRS_DEV
    block_ids = jnp.arange(NBLK, dtype=jnp.int32)
    integral_view = integrals.reshape(AUXBLK, AUX_DEV, PAIRS_DEV * OCCBLK, BS, BS)

    def one_block(total, inputs):
        block_ints, block_rows, block_cols, block_count = inputs
        live = position < block_count[owner]
        target = owner * RB + block_rows
        gathered = coeff_blocks[row_blocks[block_cols]]
        products = jnp.einsum("pkmn,kni->pkmi", block_ints.astype(jnp.float32), gathered)
        placing = ((target[:, None] == block_ids[None, :]) & live[:, None]).astype(jnp.float32)
        half = jnp.einsum("pkmi,kb->pbmi", products, placing).reshape(AUX_DEV, NBAS, O)
        half = lax.optimization_barrier(half.astype(jnp.bfloat16)).astype(jnp.float32)
        total = total + jnp.einsum("pni,pmi->nm", half, half)
        return total, None

    start = jnp.zeros((NBAS, NBAS), jnp.float32)
    total, unused = lax.scan(one_block, start, (integral_view, pair_rows, pair_cols, pair_count))
    return total
```

```python
import jax
import jax.numpy as jnp
from jax import lax
from jax.sharding import PartitionSpec as P


def contract_rows(first, second):
    return jnp.einsum("pni,pmi->nm", first, second, preferred_element_type=jnp.float32)


def local(integrals, coefficients, pair_rows, pair_cols, pair_count, row_blocks):
    aux_count, slots, block_size, _ = integrals.shape
    block_total = row_blocks.shape[0]
    occ_size = lax.axis_size("occ")
    own_blocks = block_total // occ_size
    strip_width = own_blocks * block_size
    full_coeff = lax.all_gather(coefficients, "occ", axis=0, tiled=True)
    orbitals = full_coeff.shape[1]
    coeff_blocks = full_coeff.reshape(block_total, block_size, orbitals)

    basis_block = row_blocks[pair_cols[0]]
    gathered = jnp.take(coeff_blocks, basis_block, axis=0)
    live = jnp.arange(slots, dtype=jnp.int32) < pair_count[0, 0]
    placing = (pair_rows[0][None, :] == jnp.arange(own_blocks, dtype=jnp.int32)[:, None]) & live[None, :]
    weights = jnp.where(placing[:, :, None, None], gathered[None], jnp.zeros((), gathered.dtype))
    summed_half = jnp.einsum(
        "psmn,rsni->prmi", integrals, weights, preferred_element_type=jnp.float32
    )
    half = summed_half.reshape(aux_count, strip_width, orbitals).astype(jnp.bfloat16)
    strip = contract_rows(lax.all_gather(half, "occ", axis=1, tiled=True), half)
    return lax.psum_scatter(strip, "aux", scatter_dimension=0, tiled=True)


def solution(mesh):
    return jax.shard_map(
        local,
        mesh=mesh,
        in_specs=(
            P("aux", "occ", None, None),
            P("occ", None),
            P("aux", "occ"),
            P("aux", "occ"),
            P("aux", "occ"),
            P(),
        ),
        out_specs=P("aux", "occ"),
        check_vma=False,
    )
```
